32 devices in a mesh: gx: 4 (over z), gy: 4 (over y, core), gz: 2 (over x).
Axes of the slice: x: 2, y: 2, z: 4, core: 2. Of those that a mesh axis runs over, the one named last changes fastest.
Arguments:
- offset_vector_field: float32 [3, 64, 64, 256], P(None, 'gx', 'gy', 'gz'), may hold values from -2 to 2
- earlier_creep_deformation: float32 [6, 64, 64, 256], P(None, 'gx', 'gy', 'gz'), may hold values from -0.6 to 0.6
- thermal_state: float32 [64, 64, 256], P('gx', 'gy', 'gz'), may hold values from 1 to 2
- rock_mass_per_volume: float32 [64, 64, 256], P('gx', 'gy', 'gz'), may hold values from 0.5 to 1.5
- rupture_band_indicator: int32 [64, 64, 256], P('gx', 'gy', 'gz'), may hold values 0 or 1
Outputs:
- strain_next: float32 [6, 64, 64, 256], P(None, 'gx', 'gy', 'gz')
- momentum_residual: float32 [3, 64, 64, 256], P(None, 'gx', 'gy', 'gz')
The draws below stay inside these ranges and needn't reach their ends.
All inputs are finite; a program needn't handle non-finite values. No bound on the sum of `rupture_band_indicator` on one device may be relied on, other than what follows from the above.
Results may differ from the reference program's by a relative error of at most 0.00009.
Values sent between devices are 32-bit elements; how exact they have to be, the bound alone decides.
A program may use at most 64 MiB of HBM per device.

```python
import jax
import jax.numpy as jnp
from jax import lax

TRACE_POINTS = 64
INCLINE_POINTS = 64
VERTICAL_POINTS = 256


def plant(drawn, stream_key, least, high):
    shape = drawn.shape
    index_at = [jax.random.randint(jax.random.fold_in(stream_key, axis), (), 0, shape[axis]) for axis in range(len(shape))]
    drawn = drawn.at[tuple(index_at)].set(least)
    longest = shape.index(max(shape))
    index_at[longest] = (index_at[longest] + 1) % shape[longest]
    return drawn.at[tuple(index_at)].set(high)


def steps_of(own_key, extent, cuts, low, largest):
    def one(axis_at, blocks):
        heights = jax.random.uniform(jax.random.fold_in(jax.random.fold_in(own_key, 6), axis_at), (blocks,), jnp.float32, low / len(cuts), largest / len(cuts))
        return jnp.repeat(jnp.exp(heights), extent[axis_at] // blocks).reshape((-1,) + (1,) * (len(extent) - axis_at - 1))

    loudness = one(*cuts[0])
    for cut in cuts[1:]:
        loudness = loudness * one(*cut)
    return loudness


def noise(rng, extent, spread, reach, split=(), held_as=jnp.bfloat16):
    entries = jax.random.normal(rng, extent, jnp.float32) * spread
    if len(split) > 0:
        entries = steps_of(rng, extent, split, -0.22, 0.18) * entries
    return jnp.clip(entries, min=-reach, max=reach).astype(held_as)


def setup_inputs(seed: int = 0) -> dict:
    arg_keys = jax.random.split(jax.random.key(seed), 6)
    return {
        "offset_vector_field": noise(arg_keys[0], (3, TRACE_POINTS, INCLINE_POINTS, VERTICAL_POINTS), 0.3, 2.0, ((1, 4), (2, 4), (3, 2)), jnp.float32),
        "earlier_creep_deformation": noise(arg_keys[1], (6, TRACE_POINTS, INCLINE_POINTS, VERTICAL_POINTS), 0.1, 0.6, ((1, 4), (2, 4), (3, 2)), jnp.float32),
        "thermal_state": jnp.clip(1.0 + 1.0 * jax.random.uniform(arg_keys[2], (TRACE_POINTS, INCLINE_POINTS, VERTICAL_POINTS), jnp.float32) ** steps_of(arg_keys[2], (TRACE_POINTS, INCLINE_POINTS, VERTICAL_POINTS), ((0, 4), (1, 4), (2, 2)), -0.2, 0.2), 1.0, 2.0),
        "rock_mass_per_volume": jnp.clip(0.5 + 1.0 * jax.random.uniform(arg_keys[3], (TRACE_POINTS, INCLINE_POINTS, VERTICAL_POINTS), jnp.float32) ** steps_of(arg_keys[3], (TRACE_POINTS, INCLINE_POINTS, VERTICAL_POINTS), ((0, 4), (1, 4), (2, 2)), -0.2, 0.2), 0.5, 1.5),
        "rupture_band_indicator": plant((jax.random.randint(arg_keys[4], (TRACE_POINTS, INCLINE_POINTS, VERTICAL_POINTS), 0, 8) < 1).astype(jnp.int32), jax.random.fold_in(arg_keys[4], 1), 0, 1),
    }


def central(field, axis):
    pad_list = [(0, 0), (0, 0), (0, 0)]
    pad_list[axis] = (1, 1)
    padded = jnp.pad(field, pad_list)
    length = padded.shape[axis]
    upper = lax.slice_in_dim(padded, 2, length, axis=axis)
    lower = lax.slice_in_dim(padded, 0, length - 2, axis=axis)
    return (upper - lower) * 0.5


def stress_of(elastic):
    trace = elastic[0] + elastic[1] + elastic[2]
    return [2.0 * elastic[0] + trace, 2.0 * elastic[1] + trace, 2.0 * elastic[2] + trace,
            2.0 * elastic[3], 2.0 * elastic[4], 2.0 * elastic[5]]


def evolve_deformation(deformation_parts, earlier_creep_deformation, lithostatic_load, thermal_state, rupture_band_indicator):
    traction_matrix = stress_of([deformation_parts[index] - earlier_creep_deformation[index] for index in range(6)])
    mean_stress = (traction_matrix[0] + traction_matrix[1] + traction_matrix[2]) / 3.0
    deviator = [traction_matrix[0] - mean_stress, traction_matrix[1] - mean_stress, traction_matrix[2] - mean_stress,
                traction_matrix[3], traction_matrix[4], traction_matrix[5]]
    quadratic_scalar_measure = 0.5 * (deviator[0] * deviator[0] + deviator[1] * deviator[1] + deviator[2] * deviator[2])
    quadratic_scalar_measure = quadratic_scalar_measure + deviator[3] * deviator[3] + deviator[4] * deviator[4] + deviator[5] * deviator[5]
    rupture_weakening = 1.0 + 7.0 * rupture_band_indicator.astype(jnp.float32)
    weakening_multiplier = 0.5 * rupture_weakening * jnp.exp(-(2.0 + 2.0 * lithostatic_load) / thermal_state) * quadratic_scalar_measure
    fresh_deformation = jnp.stack([earlier_creep_deformation[index] + weakening_multiplier * deviator[index] for index in range(6)])
    stress_next = stress_of([deformation_parts[index] - fresh_deformation[index] for index in range(6)])
    return fresh_deformation, stress_next


def reference(offset_vector_field, earlier_creep_deformation, thermal_state, rock_mass_per_volume, rupture_band_indicator):
    gradient = [[central(offset_vector_field[component], direction) for direction in range(3)] for component in range(3)]
    deformation_parts = [gradient[0][0], gradient[1][1], gradient[2][2],
                    0.5 * (gradient[0][1] + gradient[1][0]),
                    0.5 * (gradient[0][2] + gradient[2][0]),
                    0.5 * (gradient[1][2] + gradient[2][1])]
    depth_index = jnp.arange(VERTICAL_POINTS, dtype=jnp.float32)
    weight = rock_mass_per_volume * (1.0 + 2.0 * depth_index / VERTICAL_POINTS) / VERTICAL_POINTS
    lithostatic_load = jnp.cumsum(weight, axis=2) - 0.5 * weight
    fresh_deformation, traction_matrix = evolve_deformation(deformation_parts, earlier_creep_deformation, lithostatic_load, thermal_state, rupture_band_indicator)
    along_x = jnp.stack([central(traction_matrix[0], 0), central(traction_matrix[3], 0), central(traction_matrix[4], 0)])
    along_y = jnp.stack([central(traction_matrix[3], 1), central(traction_matrix[1], 1), central(traction_matrix[5], 1)])
    along_z = jnp.stack([central(traction_matrix[4], 2), central(traction_matrix[5], 2), central(traction_matrix[2], 2)])
    zeros = jnp.zeros_like(rock_mass_per_volume)
    momentum = along_x + along_y + along_z - jnp.stack([zeros, zeros, 0.5 * rock_mass_per_volume])
    return fresh_deformation, momentum
```

```python
import functools

import jax
import jax.numpy as jnp
from jax import lax
from jax.experimental import pallas as pl
from jax.experimental.pallas import tpu as pltpu
from jax.sharding import PartitionSpec as P

MESH = pl.DeviceIdType.MESH
AXES = ("gx", "gy", "gz")
X_SET = (0, 2, 1)
Y_SET = (2, 3, 4)
Z_SET = (1, 4, 5)


def kernel(
    dims, sizes,
    u_hbm, e_hbm, t_hbm, r_hbm, b_hbm,
    f_hbm, m_hbm,
    uv, ev, tv, rv, bv, pv, el, nt, fv, mv, sp,
    yus, yur, zus, zur, zuh, xur, yss, ysr, zss, zsr, xsr,
    in_sem, out_sem, x_send, x_recv, y_send, y_recv, z_send, z_recv,
    x2_send, x2_recv, y2_send, y2_recv, z2_send, z2_recv,
):
    X, Y, Z = dims
    N = X * Y
    layers = sizes[2]
    me = [lax.axis_index(a) for a in AXES]
    has = [(me[a] > 0, me[a] < sizes[a] - 1) for a in range(3)]

    def to(axis, step):
        return {AXES[axis]: me[axis] + step}

    loads = [
        pltpu.make_async_copy(src, dst, in_sem.at[i])
        for i, (src, dst) in enumerate(
            (
                (r_hbm, rv),
                (u_hbm, uv.at[:, pl.ds(Y, N), :]),
                (e_hbm, ev),
                (t_hbm, tv),
                (b_hbm, bv),
            )
        )
    ]
    for copy in loads:
        copy.start()

    barrier = pltpu.get_barrier_semaphore()
    expected = jnp.int32(0)
    for axis in range(3):
        for side, step in enumerate((-1, 1)):
            expected = expected + has[axis][side].astype(jnp.int32)

            @pl.when(has[axis][side])
            def _(axis=axis, step=step):
                pl.semaphore_signal(barrier, inc=1, device_id=to(axis, step), device_id_type=MESH)

    for d in range(2, layers):
        expected = expected + (me[2] + d < layers).astype(jnp.int32)

        @pl.when(me[2] >= d)
        def _(d=d):
            pl.semaphore_signal(barrier, inc=1, device_id=to(2, -d), device_id_type=MESH)

    plane = jnp.zeros((Y, Z), jnp.float32)
    for c in range(3):
        uv[c, pl.ds(0, Y), :] = plane
        uv[c, pl.ds(Y + N, Y), :] = plane
    for c in range(6):
        sp[c, pl.ds(0, Y), :] = plane
        sp[c, pl.ds(Y + N, Y), :] = plane
    for d in range(1, layers):
        @pl.when(me[2] < d)
        def _(d=d):
            zur[d - 1] = plane

    @pl.when(jnp.logical_not(has[2][0]))
    def _():
        zsr[0] = plane

    @pl.when(jnp.logical_not(has[2][1]))
    def _():
        zuh[...] = plane
        zsr[1] = plane

    lane = lax.broadcasted_iota(jnp.int32, (Y, Z), 1)
    row = lax.broadcasted_iota(jnp.int32, (Y, Z), 0)
    pair = lane >> 1
    even = (lane & 1) == 0
    not_last = jnp.where(row < Y - 1, 0.5, 0.0).astype(jnp.float32)
    not_first = jnp.where(row > 0, 0.5, 0.0).astype(jnp.float32)
    z_first = jnp.where(lane > 0, 0.5, 0.0).astype(jnp.float32)
    z_last = jnp.where(lane < Z - 1, 0.5, 0.0).astype(jnp.float32)
    z_edge = jnp.where(lane == 0, -0.5, jnp.where(lane == Z - 1, 0.5, 0.0)).astype(jnp.float32)

    loads[0].wait()
    total_depth = Z * layers
    depth = (me[2] * Z + lax.broadcasted_iota(jnp.int32, (N, Z), 1)).astype(jnp.float32)
    weight = rv[...] * (1.0 + 2.0 * depth / total_depth) / total_depth
    above_row = lax.broadcasted_iota(jnp.int32, (Z, 2 * Z), 0)
    column = lax.broadcasted_iota(jnp.int32, (Z, 2 * Z), 1)
    triangle = jnp.where(
        (above_row < column) | (column >= Z),
        1.0,
        jnp.where(above_row == column, 0.5, 0.0),
    ).astype(jnp.float32)
    sums = jnp.dot(
        weight, triangle, precision=lax.Precision.HIGHEST, preferred_element_type=jnp.float32
    )
    pv[...] = sums[:, :Z] + 1.0
    totals = sums[:, Z:]

    loads[1].wait()
    for side, y in enumerate((0, Y - 1)):
        for c in range(3):
            yus[side, c] = uv[c, pl.ds(Y + y, X, stride=Y), :]
    message = plane
    for x in range(X):
        for c in range(3):
            q = c * X + x
            tile = pltpu.roll(uv[c, pl.ds(Y + x * Y, Y), :], (2 * q + 1) % Z, 1)
            message = jnp.where(pair == q, tile, message)
        message = jnp.where(pair == 3 * X + x, totals[x * Y:(x + 1) * Y], message)
    zus[...] = message

    pl.semaphore_wait(barrier, expected)

    def remote(src, dst, send, recv, axis, step):
        return pltpu.make_async_remote_copy(
            src_ref=src, dst_ref=dst, send_sem=send, recv_sem=recv,
            device_id=to(axis, step), device_id_type=MESH,
        )

    first = []
    for side, step in enumerate((-1, 1)):
        other = 1 - side
        edge = Y if side == 0 else Y * X
        first.append((has[0][side], has[0][other], remote(
            uv.at[:, pl.ds(edge, Y), :], xur.at[other], x_send.at[side], x_recv.at[other], 0, step)))
        first.append((has[1][side], has[1][other], remote(
            yus.at[side], yur.at[other], y_send.at[side], y_recv.at[other], 1, step)))
    first.append((has[2][0], has[2][1], remote(zus, zuh, z_send.at[0], z_recv.at[0], 2, -1)))
    for d in range(1, layers):
        first.append((me[2] + d < layers, me[2] >= d, remote(
            zus, zur.at[d - 1], z_send.at[d], z_recv.at[d], 2, d)))
    for sends, _, copy in first:
        @pl.when(sends)
        def _(copy=copy):
            copy.start()

    for copy in loads[2:]:
        copy.wait()
    for x in range(X):
        base = Y + x * Y
        own = pl.ds(x * Y, Y)
        grad = []
        for c in range(3):
            here = uv[c, pl.ds(base, Y), :]
            grad.append((
                (uv[c, pl.ds(base + Y, Y), :] - uv[c, pl.ds(base - Y, Y), :]) * 0.5,
                uv[c, pl.ds(base + 1, Y), :] * not_last - uv[c, pl.ds(base - 1, Y), :] * not_first,
                pltpu.roll(here, Z - 1, 1) * z_last - pltpu.roll(here, 1, 1) * z_first,
            ))
        el[0, own, :] = grad[0][0] - ev[0, own, :]
        el[1, own, :] = grad[1][1] - ev[1, own, :]
        el[2, own, :] = grad[2][2] - ev[2, own, :]
        el[3, own, :] = 0.5 * (grad[0][1] + grad[1][0]) - ev[3, own, :]
        el[4, own, :] = 0.5 * (grad[0][2] + grad[2][0]) - ev[4, own, :]
        el[5, own, :] = 0.5 * (grad[1][2] + grad[2][1]) - ev[5, own, :]
        nt[own, :] = -2.0 / tv[own, :]

    for (_, receives, copy) in first:
        @pl.when(receives)
        def _(copy=copy):
            copy.wait_recv()

    for side in range(2):
        sign = -1.0 if side == 0 else 1.0
        at = 0 if side == 0 else X - 1
        line = 0 if side == 0 else Y - 1

        @pl.when(has[0][side])
        def _(side=side, sign=sign, at=at):
            own = pl.ds(at * Y, Y)
            for c, (part, factor) in enumerate(((0, 0.5), (3, 0.25), (4, 0.25))):
                el[part, own, :] = el[part, own, :] + (sign * factor) * xur[side, c]

        @pl.when(has[1][side])
        def _(side=side, sign=sign, line=line):
            own = pl.ds(line, X, stride=Y)
            for c, (part, factor) in enumerate(((3, 0.25), (1, 0.5), (5, 0.25))):
                el[part, own, :] = el[part, own, :] + (sign * factor) * yur[side, c]

    low = zur[0] if layers > 1 else plane
    carried = low
    for d in range(2, layers):
        carried = carried + zur[d - 1]
    merged = jnp.where(even, low, pltpu.roll(zuh[...], Z - 2, 1))

    def edge_term(tile, q):
        return (pltpu.roll(tile, (Z - 2 * q) % Z, 1) if q else tile) * z_edge

    message = plane
    for x in [0, X - 1] + list(range(1, X - 1)):
        own = pl.ds(x * Y, Y)
        e = [el[c, own, :] for c in range(6)]
        e[4] = e[4] + 0.5 * edge_term(merged, x)
        e[5] = e[5] + 0.5 * edge_term(merged, X + x)
        e[2] = e[2] + edge_term(merged, 2 * X + x)
        at = 2 * (3 * X + x)
        load = pv[own, :] + jnp.broadcast_to(carried[:, at:at + 1], (Y, Z))
        trace = e[0] + e[1] + e[2]
        third = trace * (1.0 / 3.0)
        dev = [2.0 * (e[c] - third) for c in range(3)] + [2.0 * e[c] for c in range(3, 6)]
        second = 0.5 * (dev[0] * dev[0] + dev[1] * dev[1] + dev[2] * dev[2])
        second = second + dev[3] * dev[3] + dev[4] * dev[4] + dev[5] * dev[5]
        weak = 0.5 + 3.5 * bv[own, :].astype(jnp.float32)
        rate = weak * jnp.exp(load * nt[own, :]) * second
        for c in range(6):
            step = rate * dev[c]
            fv[c, own, :] = ev[c, own, :] + step
            e[c] = e[c] - step
        trace = e[0] + e[1] + e[2]
        stress = [
            2.0 * e[0] + trace, 2.0 * e[4], 2.0 * e[3],
            2.0 * e[1] + trace, 2.0 * e[5], 2.0 * e[2] + trace,
        ]
        for c in range(6):
            sp[c, pl.ds(Y + x * Y, Y), :] = stress[c]
        for c in range(3):
            q = c * X + x
            message = jnp.where(pair == q, pltpu.roll(stress[Z_SET[c]], (2 * q + 1) % Z, 1), message)
    zss[...] = message
    for side, y in enumerate((0, Y - 1)):
        for c in range(3):
            yss[side, c] = sp[2 + c, pl.ds(Y + y, X, stride=Y), :]

    second_set = []
    for side, step in enumerate((-1, 1)):
        other = 1 - side
        edge = Y if side == 0 else Y * X
        second_set.append((has[0][side], has[0][other], remote(
            sp.at[pl.ds(0, 3), pl.ds(edge, Y), :], xsr.at[other], x2_send.at[side], x2_recv.at[other], 0, step)))
        second_set.append((has[1][side], has[1][other], remote(
            yss.at[side], ysr.at[other], y2_send.at[side], y2_recv.at[other], 1, step)))
        second_set.append((has[2][side], has[2][other], remote(
            zss, zsr.at[other], z2_send.at[side], z2_recv.at[other], 2, step)))
    for sends, _, copy in second_set:
        @pl.when(sends)
        def _(copy=copy):
            copy.start()
    strain_out = pltpu.make_async_copy(fv, f_hbm, out_sem.at[0])
    strain_out.start()

    for x in range(X):
        base = Y + x * Y
        own = pl.ds(x * Y, Y)
        for c in range(3):
            cx, cy, cz = X_SET[c], Y_SET[c], Z_SET[c]
            here = sp[cz, pl.ds(base, Y), :]
            total = (sp[cx, pl.ds(base + Y, Y), :] - sp[cx, pl.ds(base - Y, Y), :]) * 0.5
            total = total + (
                sp[cy, pl.ds(base + 1, Y), :] * not_last - sp[cy, pl.ds(base - 1, Y), :] * not_first
            )
            total = total + (pltpu.roll(here, Z - 1, 1) * z_last - pltpu.roll(here, 1, 1) * z_first)
            if c == 2:
                total = total - 0.5 * rv[own, :]
            mv[c, own, :] = total

    for (_, receives, copy) in second_set:
        @pl.when(receives)
        def _(copy=copy):
            copy.wait_recv()

    for side in range(2):
        factor = -0.5 if side == 0 else 0.5
        at = 0 if side == 0 else X - 1
        line = 0 if side == 0 else Y - 1

        @pl.when(has[0][side])
        def _(side=side, factor=factor, at=at):
            own = pl.ds(at * Y, Y)
            for c in range(3):
                mv[c, own, :] = mv[c, own, :] + factor * xsr[side, X_SET[c]]

        @pl.when(has[1][side])
        def _(side=side, factor=factor, line=line):
            own = pl.ds(line, X, stride=Y)
            for c in range(3):
                mv[c, own, :] = mv[c, own, :] + factor * ysr[side, c]

    merged = jnp.where(even, zsr[0], pltpu.roll(zsr[1], Z - 2, 1))
    for c in range(3):
        for x in range(X):
            own = pl.ds(x * Y, Y)
            mv[c, own, :] = mv[c, own, :] + edge_term(merged, c * X + x)
    residual_out = pltpu.make_async_copy(mv, m_hbm, out_sem.at[1])
    residual_out.start()

    for sends, _, copy in first + second_set:
        @pl.when(sends)
        def _(copy=copy):
            copy.wait_send()
    strain_out.wait()
    residual_out.wait()


def shards(sizes, u, e, t, r, b):
    X, Y, Z = t.shape
    N = X * Y
    layers = sizes[2]
    assert 8 * X <= Z and Z % 128 == 0 and Y % 8 == 0
    f32 = jnp.float32
    vmem = pltpu.VMEM
    dma = pltpu.SemaphoreType.DMA
    any_space = pl.BlockSpec(memory_space=pl.ANY)
    f, m = pl.pallas_call(
        functools.partial(kernel, (X, Y, Z), sizes),
        out_shape=(
            jax.ShapeDtypeStruct((6, N, Z), f32),
            jax.ShapeDtypeStruct((3, N, Z), f32),
        ),
        in_specs=[any_space] * 5,
        out_specs=(any_space, any_space),
        scratch_shapes=[
            vmem((3, N + 2 * Y, Z), f32),
            vmem((6, N, Z), f32),
            vmem((N, Z), f32),
            vmem((N, Z), f32),
            vmem((N, Z), jnp.int32),
            vmem((N, Z), f32),
            vmem((6, N, Z), f32),
            vmem((N, Z), f32),
            vmem((6, N, Z), f32),
            vmem((3, N, Z), f32),
            vmem((6, N + 2 * Y, Z), f32),
            vmem((2, 3, X, Z), f32),
            vmem((2, 3, X, Z), f32),
            vmem((Y, Z), f32),
            vmem((max(layers - 1, 1), Y, Z), f32),
            vmem((Y, Z), f32),
            vmem((2, 3, Y, Z), f32),
            vmem((2, 3, X, Z), f32),
            vmem((2, 3, X, Z), f32),
            vmem((Y, Z), f32),
            vmem((2, Y, Z), f32),
            vmem((2, 3, Y, Z), f32),
            dma((5,)),
            dma((2,)),
            dma((2,)), dma((2,)), dma((2,)), dma((2,)),
            dma((layers,)), dma((layers,)),
            dma((2,)), dma((2,)), dma((2,)), dma((2,)), dma((2,)), dma((2,)),
        ],
        compiler_params=pltpu.CompilerParams(collective_id=0, has_side_effects=True),
        name="strain_step",
    )(
        u.reshape(3, N, Z), e.reshape(6, N, Z), t.reshape(N, Z), r.reshape(N, Z), b.reshape(N, Z)
    )
    return f.reshape(6, X, Y, Z), m.reshape(3, X, Y, Z)


def solution(mesh):
    sizes = tuple(mesh.shape[a] for a in AXES)
    field = P("gx", "gy", "gz")
    fields = P(None, "gx", "gy", "gz")
    return jax.shard_map(
        functools.partial(shards, sizes),
        mesh=mesh,
        in_specs=(fields, fields, field, field, field),
        out_specs=(fields, fields),
        check_vma=False,
    )
```

```python
import functools

import jax
import jax.numpy as jnp
from jax import lax
from jax.experimental import pallas as pl
from jax.experimental.pallas import tpu as pltpu
from jax.sharding import PartitionSpec as P

MESH = pl.DeviceIdType.MESH
AXES = ("gx", "gy", "gz")
X_SET = (0, 2, 1)
Y_SET = (2, 3, 4)
Z_SET = (1, 4, 5)


def merge(pairs, Z):
    low, high = pairs[0], pairs[1]
    even = (lax.broadcasted_iota(jnp.int32, low.shape, 1) & 1) == 0
    return jnp.where(even, low, pltpu.roll(high, Z - 2, 1))


def edge_term(tile, q, z_edge):
    Z = tile.shape[1]
    return (pltpu.roll(tile, (Z - 2 * q) % Z, 1) if q else tile) * z_edge


def kernel(
    dims, sizes,
    u_hbm, e_hbm, t_hbm, r_hbm, b_hbm,
    fv, mv, zsr,
    uv, ev, tv, rv, bv, pv, el, nt, sp,
    yus, yur, zus, zur, zts, ztr, xur, yss, ysr, zss, xsr,
    in_sem, x_send, x_recv, y_send, y_recv, z_send, z_recv, t_send, t_recv,
    x2_send, x2_recv, y2_send, y2_recv, z2_send, z2_recv,
):
    X, Y, Z = dims
    N = X * Y
    layers = sizes[2]
    me = [lax.axis_index(a) for a in AXES]
    has = [(me[a] > 0, me[a] < sizes[a] - 1) for a in range(3)]

    def to(axis, step):
        return {AXES[axis]: me[axis] + step}

    loads = [
        pltpu.make_async_copy(src, dst, in_sem.at[i])
        for i, (src, dst) in enumerate(
            (
                (u_hbm, uv.at[:, pl.ds(Y, N), :]),
                (r_hbm, rv),
                (e_hbm, ev),
                (t_hbm, tv),
                (b_hbm, bv),
            )
        )
    ]
    for copy in loads:
        copy.start()

    barrier = pltpu.get_barrier_semaphore()
    expected = jnp.int32(0)
    for axis in range(3):
        for side, step in enumerate((-1, 1)):
            expected = expected + has[axis][side].astype(jnp.int32)

            @pl.when(has[axis][side])
            def _(axis=axis, step=step):
                pl.semaphore_signal(barrier, inc=1, device_id=to(axis, step), device_id_type=MESH)

    for d in range(2, layers):
        expected = expected + (me[2] + d < layers).astype(jnp.int32)

        @pl.when(me[2] >= d)
        def _(d=d):
            pl.semaphore_signal(barrier, inc=1, device_id=to(2, -d), device_id_type=MESH)

    plane = jnp.zeros((Y, Z), jnp.float32)
    for c in range(3):
        uv[c, pl.ds(0, Y), :] = plane
        uv[c, pl.ds(Y + N, Y), :] = plane
    for c in range(6):
        sp[c, pl.ds(0, Y), :] = plane
        sp[c, pl.ds(Y + N, Y), :] = plane
    for d in range(1, layers):
        @pl.when(me[2] < d)
        def _(d=d):
            ztr[d - 1] = plane

    for side in range(2):
        @pl.when(jnp.logical_not(has[2][side]))
        def _(side=side):
            zur[side] = plane
            zsr[side] = plane

    lane = lax.broadcasted_iota(jnp.int32, (Y, Z), 1)
    row = lax.broadcasted_iota(jnp.int32, (Y, Z), 0)
    pair = lane >> 1
    not_last = jnp.where(row < Y - 1, 0.5, 0.0).astype(jnp.float32)
    not_first = jnp.where(row > 0, 0.5, 0.0).astype(jnp.float32)
    z_first = jnp.where(lane > 0, 0.5, 0.0).astype(jnp.float32)
    z_last = jnp.where(lane < Z - 1, 0.5, 0.0).astype(jnp.float32)
    z_edge = jnp.where(lane == 0, -0.5, jnp.where(lane == Z - 1, 0.5, 0.0)).astype(jnp.float32)

    def remote(src, dst, send, recv, axis, step):
        return pltpu.make_async_remote_copy(
            src_ref=src, dst_ref=dst, send_sem=send, recv_sem=recv,
            device_id=to(axis, step), device_id_type=MESH,
        )

    def start(copies):
        for sends, _, copy in copies:
            @pl.when(sends)
            def _(copy=copy):
                copy.start()

    def arrive(copies):
        for _, receives, copy in copies:
            @pl.when(receives)
            def _(copy=copy):
                copy.wait_recv()

    def faces(axis, src, dst, send, recv):
        return [
            (has[axis][side], has[axis][1 - side], remote(
                src[side], dst.at[1 - side], send.at[side], recv.at[1 - side], axis, step))
            for side, step in enumerate((-1, 1))
        ]

    edges = (pl.ds(Y, Y), pl.ds(Y * X, Y))
    u_x = faces(0, [uv.at[:, edge, :] for edge in edges], xur, x_send, x_recv)
    u_y = faces(1, [yus.at[0], yus.at[1]], yur, y_send, y_recv)
    u_z = faces(2, [zus, zus], zur, z_send, z_recv)
    totals_down = [
        (me[2] + d < layers, me[2] >= d, remote(
            zts, ztr.at[d - 1], t_send.at[d - 1], t_recv.at[d - 1], 2, d))
        for d in range(1, layers)
    ]

    loads[0].wait()
    for side, y in enumerate((0, Y - 1)):
        for c in range(3):
            yus[side, c] = uv[c, pl.ds(Y + y, X, stride=Y), :]
    message = plane
    for x in range(X):
        for c in range(3):
            q = c * X + x
            tile = pltpu.roll(uv[c, pl.ds(Y + x * Y, Y), :], (2 * q + 1) % Z, 1)
            message = jnp.where(pair == q, tile, message)
    zus[...] = message
    pl.semaphore_wait(barrier, expected)
    start(u_z + u_x + u_y)

    loads[1].wait()
    total_depth = Z * layers
    depth = (me[2] * Z + lax.broadcasted_iota(jnp.int32, (N, Z), 1)).astype(jnp.float32)
    weight = rv[...] * (1.0 + 2.0 * depth / total_depth) / total_depth
    above_row = lax.broadcasted_iota(jnp.int32, (Z, 2 * Z), 0)
    column = lax.broadcasted_iota(jnp.int32, (Z, 2 * Z), 1)
    triangle = jnp.where(
        (above_row < column) | (column >= Z),
        1.0,
        jnp.where(above_row == column, 0.5, 0.0),
    ).astype(jnp.float32)
    sums = jnp.dot(
        weight, triangle, precision=lax.Precision.HIGHEST, preferred_element_type=jnp.float32
    )
    pv[...] = sums[:, :Z] + 1.0
    totals = sums[:, Z:]
    message = plane
    for x in range(X):
        message = jnp.where(lane == x, totals[x * Y:(x + 1) * Y], message)
    zts[...] = message
    start(totals_down)

    for copy in loads[2:]:
        copy.wait()
    for x in range(X):
        base = Y + x * Y
        own = pl.ds(x * Y, Y)
        grad = []
        for c in range(3):
            here = uv[c, pl.ds(base, Y), :]
            grad.append((
                (uv[c, pl.ds(base + Y, Y), :] - uv[c, pl.ds(base - Y, Y), :]) * 0.5,
                uv[c, pl.ds(base + 1, Y), :] * not_last - uv[c, pl.ds(base - 1, Y), :] * not_first,
                pltpu.roll(here, Z - 1, 1) * z_last - pltpu.roll(here, 1, 1) * z_first,
            ))
        el[0, own, :] = grad[0][0] - ev[0, own, :]
        el[1, own, :] = grad[1][1] - ev[1, own, :]
        el[2, own, :] = grad[2][2] - ev[2, own, :]
        el[3, own, :] = 0.5 * (grad[0][1] + grad[1][0]) - ev[3, own, :]
        el[4, own, :] = 0.5 * (grad[0][2] + grad[2][0]) - ev[4, own, :]
        el[5, own, :] = 0.5 * (grad[1][2] + grad[2][1]) - ev[5, own, :]
        nt[own, :] = -2.0 / tv[own, :]

    arrive(u_x + u_y)
    for side in range(2):
        sign = -1.0 if side == 0 else 1.0
        at = 0 if side == 0 else X - 1
        line = 0 if side == 0 else Y - 1

        @pl.when(has[0][side])
        def _(side=side, sign=sign, at=at):
            own = pl.ds(at * Y, Y)
            for c, (part, factor) in enumerate(((0, 0.5), (3, 0.25), (4, 0.25))):
                el[part, own, :] = el[part, own, :] + (sign * factor) * xur[side, c]

        @pl.when(has[1][side])
        def _(side=side, sign=sign, line=line):
            own = pl.ds(line, X, stride=Y)
            for c, (part, factor) in enumerate(((3, 0.25), (1, 0.5), (5, 0.25))):
                el[part, own, :] = el[part, own, :] + (sign * factor) * yur[side, c]

    arrive(totals_down + u_z)
    carried = plane
    for d in range(1, layers):
        carried = carried + ztr[d - 1]
    merged = merge(zur, Z)

    s_x = faces(0, [sp.at[pl.ds(0, 3), edge, :] for edge in edges], xsr, x2_send, x2_recv)
    s_y = faces(1, [yss.at[0], yss.at[1]], ysr, y2_send, y2_recv)
    s_z = faces(2, [zss, zss], zsr, z2_send, z2_recv)

    message = plane
    for step, x in enumerate([0, X - 1] + list(range(1, X - 1))):
        own = pl.ds(x * Y, Y)
        e = [el[c, own, :] for c in range(6)]
        e[4] = e[4] + 0.5 * edge_term(merged, x, z_edge)
        e[5] = e[5] + 0.5 * edge_term(merged, X + x, z_edge)
        e[2] = e[2] + edge_term(merged, 2 * X + x, z_edge)
        load = pv[own, :] + jnp.broadcast_to(carried[:, x:x + 1], (Y, Z))
        trace = e[0] + e[1] + e[2]
        third = trace * (1.0 / 3.0)
        half = [e[0] - third, e[1] - third, e[2] - third, e[3], e[4], e[5]]
        second = half[0] * half[0] + half[1] * half[1] + half[2] * half[2]
        second = second + 2.0 * (half[3] * half[3] + half[4] * half[4] + half[5] * half[5])
        weak = 2.0 + 14.0 * bv[own, :].astype(jnp.float32)
        rate = weak * jnp.exp(load * nt[own, :]) * second
        for c in range(6):
            change = rate * half[c]
            fv[c, own, :] = ev[c, own, :] + change
            e[c] = e[c] - change
        trace = e[0] + e[1] + e[2]
        stress = [
            2.0 * e[0] + trace, 2.0 * e[4], 2.0 * e[3],
            2.0 * e[1] + trace, 2.0 * e[5], 2.0 * e[2] + trace,
        ]
        for c in range(6):
            sp[c, pl.ds(Y + x * Y, Y), :] = stress[c]
        for c in range(3):
            q = c * X + x
            message = jnp.where(pair == q, pltpu.roll(stress[Z_SET[c]], (2 * q + 1) % Z, 1), message)
        if step == 1:
            start(s_x)
    zss[...] = message
    start(s_z)
    for side, y in enumerate((0, Y - 1)):
        for c in range(3):
            yss[side, c] = sp[2 + c, pl.ds(Y + y, X, stride=Y), :]
    start(s_y)

    for x in range(X):
        base = Y + x * Y
        own = pl.ds(x * Y, Y)
        for c in range(3):
            cx, cy, cz = X_SET[c], Y_SET[c], Z_SET[c]
            here = sp[cz, pl.ds(base, Y), :]
            total = (sp[cx, pl.ds(base + Y, Y), :] - sp[cx, pl.ds(base - Y, Y), :]) * 0.5
            total = total + (
                sp[cy, pl.ds(base + 1, Y), :] * not_last - sp[cy, pl.ds(base - 1, Y), :] * not_first
            )
            total = total + (pltpu.roll(here, Z - 1, 1) * z_last - pltpu.roll(here, 1, 1) * z_first)
            if c == 2:
                total = total - 0.5 * rv[own, :]
            mv[c, own, :] = total

    arrive(s_x + s_y)
    for side in range(2):
        factor = -0.5 if side == 0 else 0.5
        at = 0 if side == 0 else X - 1
        line = 0 if side == 0 else Y - 1

        @pl.when(has[0][side])
        def _(side=side, factor=factor, at=at):
            own = pl.ds(at * Y, Y)
            for c in range(3):
                mv[c, own, :] = mv[c, own, :] + factor * xsr[side, X_SET[c]]

        @pl.when(has[1][side])
        def _(side=side, factor=factor, line=line):
            own = pl.ds(line, X, stride=Y)
            for c in range(3):
                mv[c, own, :] = mv[c, own, :] + factor * ysr[side, c]

    arrive(s_z)
    for sends, _, copy in u_x + u_y + u_z + totals_down + s_x + s_y + s_z:
        @pl.when(sends)
        def _(copy=copy):
            copy.wait_send()


def finish(dims, fv, mv, zsr, f_hbm, m_hbm, mo, sem):
    X, Y, Z = dims
    N = X * Y
    strain_out = pltpu.make_async_copy(fv, f_hbm, sem.at[3])
    strain_out.start()
    lane = lax.broadcasted_iota(jnp.int32, (Y, Z), 1)
    z_edge = jnp.where(lane == 0, -0.5, jnp.where(lane == Z - 1, 0.5, 0.0)).astype(jnp.float32)
    merged = merge(zsr, Z)
    outs = []
    for c in range(3):
        for x in range(X):
            own = pl.ds(x * Y, Y)
            mo[c, own, :] = mv[c, own, :] + edge_term(merged, c * X + x, z_edge)
        outs.append(pltpu.make_async_copy(mo.at[c], m_hbm.at[c], sem.at[c]))
        outs[c].start()
    for copy in outs:
        copy.wait()
    strain_out.wait()


def shards(sizes, u, e, t, r, b):
    X, Y, Z = t.shape
    N = X * Y
    layers = sizes[2]
    assert 8 * X <= Z and Z % 128 == 0 and Y % 8 == 0
    f32 = jnp.float32
    vmem = pltpu.VMEM
    dma = pltpu.SemaphoreType.DMA
    any_space = pl.BlockSpec(memory_space=pl.ANY)
    in_vmem = pl.BlockSpec(memory_space=vmem)
    pair_sem = dma((2,))
    per_layer = dma((max(layers - 1, 1),))
    kept = pl.pallas_call(
        functools.partial(kernel, (X, Y, Z), sizes),
        out_shape=(vmem((6, N, Z), f32), vmem((3, N, Z), f32), vmem((2, Y, Z), f32)),
        in_specs=[any_space] * 5,
        out_specs=(in_vmem, in_vmem, in_vmem),
        scratch_shapes=[
            vmem((3, N + 2 * Y, Z), f32),
            vmem((6, N, Z), f32),
            vmem((N, Z), f32),
            vmem((N, Z), f32),
            vmem((N, Z), jnp.int32),
            vmem((N, Z), f32),
            vmem((6, N, Z), f32),
            vmem((N, Z), f32),
            vmem((6, N + 2 * Y, Z), f32),
            vmem((2, 3, X, Z), f32),
            vmem((2, 3, X, Z), f32),
            vmem((Y, Z), f32),
            vmem((2, Y, Z), f32),
            vmem((Y, Z), f32),
            vmem((max(layers - 1, 1), Y, Z), f32),
            vmem((2, 3, Y, Z), f32),
            vmem((2, 3, X, Z), f32),
            vmem((2, 3, X, Z), f32),
            vmem((Y, Z), f32),
            vmem((2, 3, Y, Z), f32),
            dma((5,)),
        ] + [pair_sem] * 6 + [per_layer] * 2 + [pair_sem] * 6,
        compiler_params=pltpu.CompilerParams(collective_id=0, has_side_effects=True),
        name="strain_step",
    )(
        u.reshape(3, N, Z), e.reshape(6, N, Z), t.reshape(N, Z), r.reshape(N, Z), b.reshape(N, Z)
    )
    f, m = pl.pallas_call(
        functools.partial(finish, (X, Y, Z)),
        out_shape=(jax.ShapeDtypeStruct((6, N, Z), f32), jax.ShapeDtypeStruct((3, N, Z), f32)),
        in_specs=[in_vmem] * 3,
        out_specs=(any_space, any_space),
        scratch_shapes=[vmem((3, N, Z), f32), dma((4,))],
        name="finish",
    )(*(pltpu.with_memory_space_constraint(k, vmem) for k in kept))
    return f.reshape(6, X, Y, Z), m.reshape(3, X, Y, Z)


def solution(mesh):
    sizes = tuple(mesh.shape[a] for a in AXES)
    field = P("gx", "gy", "gz")
    fields = P(None, "gx", "gy", "gz")
    return jax.shard_map(
        functools.partial(shards, sizes),
        mesh=mesh,
        in_specs=(fields, fields, field, field, field),
        out_specs=(fields, fields),
        check_vma=False,
    )
```

```python
import functools

import jax
import jax.numpy as jnp
from jax import lax
from jax.experimental import pallas as pl
from jax.experimental.pallas import tpu as pltpu
from jax.sharding import PartitionSpec as P

MESH = pl.DeviceIdType.MESH
AXES = ("gx", "gy", "gz")
X_SET = (0, 2, 1)
Y_SET = (2, 3, 4)
Z_SET = (1, 4, 5)


def merge(pairs, Z):
    low, high = pairs[0], pairs[1]
    even = (lax.broadcasted_iota(jnp.int32, low.shape, 1) & 1) == 0
    return jnp.where(even, low, pltpu.roll(high, Z - 2, 1))


def edge_term(tile, q, z_edge):
    Z = tile.shape[1]
    return (pltpu.roll(tile, (Z - 2 * q) % Z, 1) if q else tile) * z_edge


def kernel(
    dims, sizes,
    u_hbm, u_rows, e_hbm, t_hbm, r_hbm, b_hbm,
    fv, mv,
    uv, ev, tv, rv, bv, pv, el, nt, sp,
    yur, zus, zur, zts, ztr, xur, yss, ysr, zss, zsr, xsr,
    in_sem, x_send, x_recv, y_send, y_recv, z_send, z_recv, t_send, t_recv,
    x2_send, x2_recv, y2_send, y2_recv, z2_send, z2_recv,
):
    X, Y, Z = dims
    N = X * Y
    layers = sizes[2]
    me = [lax.axis_index(a) for a in AXES]
    has = [(me[a] > 0, me[a] < sizes[a] - 1) for a in range(3)]

    def to(axis, step):
        return {AXES[axis]: me[axis] + step}

    loads = [
        pltpu.make_async_copy(src, dst, in_sem.at[i])
        for i, (src, dst) in enumerate(
            (
                (u_hbm, uv.at[:, pl.ds(Y, N), :]),
                (r_hbm, rv),
                (e_hbm, ev),
                (t_hbm, tv),
                (b_hbm, bv),
            )
        )
    ]
    for copy in loads:
        copy.start()

    barrier = pltpu.get_barrier_semaphore()
    expected = jnp.int32(0)
    for axis in range(3):
        for side, step in enumerate((-1, 1)):
            expected = expected + has[axis][side].astype(jnp.int32)

            @pl.when(has[axis][side])
            def _(axis=axis, step=step):
                pl.semaphore_signal(barrier, inc=1, device_id=to(axis, step), device_id_type=MESH)

    for d in range(2, layers):
        expected = expected + (me[2] + d < layers).astype(jnp.int32)

        @pl.when(me[2] >= d)
        def _(d=d):
            pl.semaphore_signal(barrier, inc=1, device_id=to(2, -d), device_id_type=MESH)

    plane = jnp.zeros((Y, Z), jnp.float32)
    for c in range(3):
        uv[c, pl.ds(0, Y), :] = plane
        uv[c, pl.ds(Y + N, Y), :] = plane
    for c in range(6):
        sp[c, pl.ds(0, Y), :] = plane
        sp[c, pl.ds(Y + N, Y), :] = plane
    for d in range(1, layers):
        @pl.when(me[2] < d)
        def _(d=d):
            ztr[d - 1] = plane

    for side in range(2):
        @pl.when(jnp.logical_not(has[2][side]))
        def _(side=side):
            zur[side] = plane
            zsr[side] = plane

        @pl.when(jnp.logical_not(has[1][side]))
        def _(side=side):
            for c in range(3):
                yur[side, c] = jnp.zeros((X, Z), jnp.float32)

    lane = lax.broadcasted_iota(jnp.int32, (Y, Z), 1)
    row = lax.broadcasted_iota(jnp.int32, (Y, Z), 0)
    pair = lane >> 1
    not_last = jnp.where(row < Y - 1, 0.5, 0.0).astype(jnp.float32)
    not_first = jnp.where(row > 0, 0.5, 0.0).astype(jnp.float32)
    z_first = jnp.where(lane > 0, 0.5, 0.0).astype(jnp.float32)
    z_last = jnp.where(lane < Z - 1, 0.5, 0.0).astype(jnp.float32)
    z_edge = jnp.where(lane == 0, -0.5, jnp.where(lane == Z - 1, 0.5, 0.0)).astype(jnp.float32)

    def remote(src, dst, send, recv, axis, step):
        return pltpu.make_async_remote_copy(
            src_ref=src, dst_ref=dst, send_sem=send, recv_sem=recv,
            device_id=to(axis, step), device_id_type=MESH,
        )

    def start(copies):
        for sends, _, copy in copies:
            @pl.when(sends)
            def _(copy=copy):
                copy.start()

    def arrive(copies):
        for _, receives, copy in copies:
            @pl.when(receives)
            def _(copy=copy):
                copy.wait_recv()

    def faces(axis, src, dst, send, recv):
        return [
            (has[axis][side], has[axis][1 - side], remote(
                src[side], dst.at[1 - side], send.at[side], recv.at[1 - side], axis, step))
            for side, step in enumerate((-1, 1))
        ]

    edges = (pl.ds(Y, Y), pl.ds(Y * X, Y))
    u_x = faces(0, [u_hbm.at[:, pl.ds(at, Y), :] for at in (0, N - Y)], xur, x_send, x_recv)
    u_y = faces(1, [u_rows.at[:, :, y, :] for y in (0, Y - 1)], yur, y_send, y_recv)
    u_z = faces(2, [zus, zus], zur, z_send, z_recv)
    totals_down = [
        (me[2] + d < layers, me[2] >= d, remote(
            zts, ztr.at[d - 1], t_send.at[d - 1], t_recv.at[d - 1], 2, d))
        for d in range(1, layers)
    ]

    pl.semaphore_wait(barrier, expected)
    start(u_y + u_x)
    loads[0].wait()
    message = plane
    for x in range(X):
        for c in range(3):
            q = c * X + x
            tile = pltpu.roll(uv[c, pl.ds(Y + x * Y, Y), :], (2 * q + 1) % Z, 1)
            message = jnp.where(pair == q, tile, message)
    zus[...] = message
    start(u_z)

    loads[1].wait()
    total_depth = Z * layers
    depth = (me[2] * Z + lax.broadcasted_iota(jnp.int32, (N, Z), 1)).astype(jnp.float32)
    weight = rv[...] * (1.0 + 2.0 * depth / total_depth) / total_depth
    above_row = lax.broadcasted_iota(jnp.int32, (Z, 2 * Z), 0)
    column = lax.broadcasted_iota(jnp.int32, (Z, 2 * Z), 1)
    triangle = jnp.where(
        (above_row < column) | (column >= Z),
        1.0,
        jnp.where(above_row == column, 0.5, 0.0),
    ).astype(jnp.float32)
    sums = jnp.dot(
        weight, triangle, precision=lax.Precision.HIGHEST, preferred_element_type=jnp.float32
    )
    pv[...] = sums[:, :Z] + 1.0
    totals = sums[:, Z:]
    message = plane
    for x in range(X):
        message = jnp.where(lane == x, totals[x * Y:(x + 1) * Y], message)
    zts[...] = message
    start(totals_down)

    for copy in loads[2:]:
        copy.wait()
    for x in range(X):
        base = Y + x * Y
        own = pl.ds(x * Y, Y)
        grad = []
        for c in range(3):
            here = uv[c, pl.ds(base, Y), :]
            grad.append((
                (uv[c, pl.ds(base + Y, Y), :] - uv[c, pl.ds(base - Y, Y), :]) * 0.5,
                uv[c, pl.ds(base + 1, Y), :] * not_last - uv[c, pl.ds(base - 1, Y), :] * not_first,
                pltpu.roll(here, Z - 1, 1) * z_last - pltpu.roll(here, 1, 1) * z_first,
            ))
        el[0, own, :] = grad[0][0] - ev[0, own, :]
        el[1, own, :] = grad[1][1] - ev[1, own, :]
        el[2, own, :] = grad[2][2] - ev[2, own, :]
        el[3, own, :] = 0.5 * (grad[0][1] + grad[1][0]) - ev[3, own, :]
        el[4, own, :] = 0.5 * (grad[0][2] + grad[2][0]) - ev[4, own, :]
        el[5, own, :] = 0.5 * (grad[1][2] + grad[2][1]) - ev[5, own, :]
        nt[own, :] = -2.0 / tv[own, :]

    arrive(u_x)
    for side, at in enumerate((0, X - 1)):
        sign = 2.0 * side - 1.0

        @pl.when(has[0][side])
        def _(side=side, sign=sign, at=at):
            own = pl.ds(at * Y, Y)
            for c, (part, factor) in enumerate(((0, 0.5), (3, 0.25), (4, 0.25))):
                el[part, own, :] = el[part, own, :] + (sign * factor) * xur[side, c]

    arrive(u_z + totals_down)
    carried = plane
    for d in range(1, layers):
        carried = carried + ztr[d - 1]
    merged = merge(zur, Z)

    s_x = faces(0, [sp.at[pl.ds(0, 3), edge, :] for edge in edges], xsr, x2_send, x2_recv)
    s_y = faces(1, [yss.at[0], yss.at[1]], ysr, y2_send, y2_recv)
    s_z = faces(2, [zss, zss], zsr, z2_send, z2_recv)

    def evolve(e, load, own):
        trace = e[0] + e[1] + e[2]
        third = trace * (1.0 / 3.0)
        half = [e[0] - third, e[1] - third, e[2] - third, e[3], e[4], e[5]]
        second = half[0] * half[0] + half[1] * half[1] + half[2] * half[2]
        second = second + 2.0 * (half[3] * half[3] + half[4] * half[4] + half[5] * half[5])
        weak = 2.0 + 14.0 * bv[own, :].astype(jnp.float32)
        rate = weak * jnp.exp(load * nt[own, :]) * second
        e = list(e)
        for c in range(6):
            change = rate * half[c]
            fv[c, own, :] = ev[c, own, :] + change
            e[c] = e[c] - change
        trace = e[0] + e[1] + e[2]
        return [
            2.0 * e[0] + trace, 2.0 * e[4], 2.0 * e[3],
            2.0 * e[1] + trace, 2.0 * e[5], 2.0 * e[2] + trace,
        ]

    for x in range(X):
        own = pl.ds(x * Y, Y)
        e = [el[c, own, :] for c in range(6)]
        e[4] = e[4] + 0.5 * edge_term(merged, x, z_edge)
        e[5] = e[5] + 0.5 * edge_term(merged, X + x, z_edge)
        e[2] = e[2] + edge_term(merged, 2 * X + x, z_edge)
        for c in (2, 4, 5):
            el[c, own, :] = e[c]
        load = pv[own, :] + jnp.broadcast_to(carried[:, x:x + 1], (Y, Z))
        pv[own, :] = load
        stress = evolve(e, load, own)
        for c in range(6):
            sp[c, pl.ds(Y + x * Y, Y), :] = stress[c]

    arrive(u_y)
    for side, line in enumerate((0, Y - 1)):
        sign = 2.0 * side - 1.0
        own = pl.ds(line, X, stride=Y)
        e = [el[c, own, :] for c in range(6)]
        for c, (part, factor) in enumerate(((3, 0.25), (1, 0.5), (5, 0.25))):
            e[part] = e[part] + (sign * factor) * yur[side, c]
        stress = evolve(e, pv[own, :], own)
        for c in range(3):
            yss[side, c] = stress[Y_SET[c]]
        for c in range(6):
            sp[c, pl.ds(Y + line, X, stride=Y), :] = stress[c]
    start(s_y + s_x)
    message = plane
    for x in range(X):
        for c in range(3):
            q = c * X + x
            tile = pltpu.roll(sp[Z_SET[c], pl.ds(Y + x * Y, Y), :], (2 * q + 1) % Z, 1)
            message = jnp.where(pair == q, tile, message)
    zss[...] = message
    start(s_z)

    for x in range(X):
        base = Y + x * Y
        own = pl.ds(x * Y, Y)
        for c in range(3):
            cx, cy, cz = X_SET[c], Y_SET[c], Z_SET[c]
            here = sp[cz, pl.ds(base, Y), :]
            total = (sp[cx, pl.ds(base + Y, Y), :] - sp[cx, pl.ds(base - Y, Y), :]) * 0.5
            total = total + (
                sp[cy, pl.ds(base + 1, Y), :] * not_last - sp[cy, pl.ds(base - 1, Y), :] * not_first
            )
            total = total + (pltpu.roll(here, Z - 1, 1) * z_last - pltpu.roll(here, 1, 1) * z_first)
            if c == 2:
                total = total - 0.5 * rv[own, :]
            mv[c, own, :] = total

    arrive(s_x)
    for side, at in enumerate((0, X - 1)):
        @pl.when(has[0][side])
        def _(side=side, at=at):
            own = pl.ds(at * Y, Y)
            for c in range(3):
                mv[c, own, :] = mv[c, own, :] + (side - 0.5) * xsr[side, X_SET[c]]

    arrive(s_z)
    merged = merge(zsr, Z)
    for c in range(3):
        for x in range(X):
            own = pl.ds(x * Y, Y)
            mv[c, own, :] = mv[c, own, :] + edge_term(merged, c * X + x, z_edge)

    for sends, _, copy in u_x + u_y + u_z + totals_down + s_x + s_z:
        @pl.when(sends)
        def _(copy=copy):
            copy.wait_send()

    arrive(s_y)
    for side, line in enumerate((0, Y - 1)):
        @pl.when(has[1][side])
        def _(side=side, line=line):
            own = pl.ds(line, X, stride=Y)
            for c in range(3):
                mv[c, own, :] = mv[c, own, :] + (side - 0.5) * ysr[side, c]

    for sends, _, copy in s_y:
        @pl.when(sends)
        def _(copy=copy):
            copy.wait_send()


def finish(fv, mv, f_hbm, m_hbm, sem):
    copies = [
        pltpu.make_async_copy(mv, m_hbm, sem.at[0]),
        pltpu.make_async_copy(fv, f_hbm, sem.at[1]),
    ]
    for copy in copies:
        copy.start()
    for copy in copies:
        copy.wait()


def shards(sizes, u, e, t, r, b):
    X, Y, Z = t.shape
    N = X * Y
    layers = sizes[2]
    assert 8 * X <= Z and Z % 128 == 0 and Y % 8 == 0
    f32 = jnp.float32
    vmem = pltpu.VMEM
    dma = pltpu.SemaphoreType.DMA
    any_space = pl.BlockSpec(memory_space=pl.ANY)
    in_vmem = pl.BlockSpec(memory_space=vmem)
    pair_sem = dma((2,))
    per_layer = dma((max(layers - 1, 1),))
    kept = pl.pallas_call(
        functools.partial(kernel, (X, Y, Z), sizes),
        out_shape=(vmem((6, N, Z), f32), vmem((3, N, Z), f32)),
        in_specs=[any_space] * 6,
        out_specs=(in_vmem, in_vmem),
        scratch_shapes=[
            vmem((3, N + 2 * Y, Z), f32),
            vmem((6, N, Z), f32),
            vmem((N, Z), f32),
            vmem((N, Z), f32),
            vmem((N, Z), jnp.int32),
            vmem((N, Z), f32),
            vmem((6, N, Z), f32),
            vmem((N, Z), f32),
            vmem((6, N + 2 * Y, Z), f32),
            vmem((2, 3, X, Z), f32),
            vmem((Y, Z), f32),
            vmem((2, Y, Z), f32),
            vmem((Y, Z), f32),
            vmem((max(layers - 1, 1), Y, Z), f32),
            vmem((2, 3, Y, Z), f32),
            vmem((2, 3, X, Z), f32),
            vmem((2, 3, X, Z), f32),
            vmem((Y, Z), f32),
            vmem((2, Y, Z), f32),
            vmem((2, 3, Y, Z), f32),
            dma((5,)),
        ] + [pair_sem] * 6 + [per_layer] * 2 + [pair_sem] * 6,
        compiler_params=pltpu.CompilerParams(collective_id=0, has_side_effects=True),
        name="strain_step",
    )(
        u.reshape(3, N, Z), u, e.reshape(6, N, Z), t.reshape(N, Z), r.reshape(N, Z), b.reshape(N, Z)
    )
    f, m = pl.pallas_call(
        finish,
        out_shape=(jax.ShapeDtypeStruct((6, N, Z), f32), jax.ShapeDtypeStruct((3, N, Z), f32)),
        in_specs=[in_vmem] * 2,
        out_specs=(any_space, any_space),
        scratch_shapes=[pair_sem],
        name="finish",
    )(*(pltpu.with_memory_space_constraint(k, vmem) for k in kept))
    return f.reshape(6, X, Y, Z), m.reshape(3, X, Y, Z)


def solution(mesh):
    sizes = tuple(mesh.shape[a] for a in AXES)
    field = P("gx", "gy", "gz")
    fields = P(None, "gx", "gy", "gz")
    return jax.shard_map(
        functools.partial(shards, sizes),
        mesh=mesh,
        in_specs=(fields, fields, field, field, field),
        out_specs=(fields, fields),
        check_vma=False,
    )
```

```python
import functools

import jax
import jax.numpy as jnp
from jax import lax
from jax.experimental import pallas as pl
from jax.experimental.pallas import tpu as pltpu
from jax.sharding import PartitionSpec as P

MESH = pl.DeviceIdType.MESH
AXES = ("gx", "gy", "gz")
X_SET = (0, 2, 1)
Y_SET = (2, 3, 4)
Z_SET = (1, 4, 5)


def merge(pairs, Z):
    low, high = pairs[0], pairs[1]
    even = (lax.broadcasted_iota(jnp.int32, low.shape, 1) & 1) == 0
    return jnp.where(even, low, pltpu.roll(high, Z - 2, 1))


def edge_term(tile, q, z_edge):
    Z = tile.shape[1]
    return (pltpu.roll(tile, (Z - 2 * q) % Z, 1) if q else tile) * z_edge


def kernel(
    dims, sizes,
    u_hbm, u_rows, e_hbm, t_hbm, r_hbm, b_hbm,
    fv, mv,
    uv, ev, tv, rv, bv, pv, el, nt, sp,
    yur, zus, zur, zts, ztr, xur, yss, ysr, zss, zsr, xsr,
    in_sem, x_send, x_recv, y_send, y_recv, z_send, z_recv, t_send, t_recv,
    x2_send, x2_recv, y2_send, y2_recv, z2_send, z2_recv,
):
    X, Y, Z = dims
    N = X * Y
    layers = sizes[2]
    me = [lax.axis_index(a) for a in AXES]
    has = [(me[a] > 0, me[a] < sizes[a] - 1) for a in range(3)]

    def to(axis, step):
        return {AXES[axis]: me[axis] + step}

    loads = [
        pltpu.make_async_copy(src, dst, in_sem.at[i])
        for i, (src, dst) in enumerate(
            (
                (u_hbm, uv.at[:, pl.ds(Y, N), :]),
                (r_hbm, rv),
                (e_hbm, ev),
                (t_hbm, tv),
                (b_hbm, bv),
            )
        )
    ]
    for copy in loads:
        copy.start()

    barrier = pltpu.get_barrier_semaphore()
    expected = jnp.int32(0)
    for axis in range(3):
        for side, step in enumerate((-1, 1)):
            expected = expected + has[axis][side].astype(jnp.int32)

            @pl.when(has[axis][side])
            def _(axis=axis, step=step):
                pl.semaphore_signal(barrier, inc=1, device_id=to(axis, step), device_id_type=MESH)

    for d in range(2, layers):
        expected = expected + (me[2] + d < layers).astype(jnp.int32)

        @pl.when(me[2] >= d)
        def _(d=d):
            pl.semaphore_signal(barrier, inc=1, device_id=to(2, -d), device_id_type=MESH)

    plane = jnp.zeros((Y, Z), jnp.float32)
    for c in range(3):
        uv[c, pl.ds(0, Y), :] = plane
        uv[c, pl.ds(Y + N, Y), :] = plane
    for c in range(6):
        sp[c, pl.ds(0, Y), :] = plane
        sp[c, pl.ds(Y + N, Y), :] = plane
    for d in range(1, layers):
        @pl.when(me[2] < d)
        def _(d=d):
            ztr[d - 1] = plane

    for side in range(2):
        @pl.when(jnp.logical_not(has[2][side]))
        def _(side=side):
            zur[side] = plane
            zsr[side] = plane

    lane = lax.broadcasted_iota(jnp.int32, (Y, Z), 1)
    row = lax.broadcasted_iota(jnp.int32, (Y, Z), 0)
    pair = lane >> 1
    not_last = jnp.where(row < Y - 1, 0.5, 0.0).astype(jnp.float32)
    not_first = jnp.where(row > 0, 0.5, 0.0).astype(jnp.float32)
    z_first = jnp.where(lane > 0, 0.5, 0.0).astype(jnp.float32)
    z_last = jnp.where(lane < Z - 1, 0.5, 0.0).astype(jnp.float32)
    z_edge = jnp.where(lane == 0, -0.5, jnp.where(lane == Z - 1, 0.5, 0.0)).astype(jnp.float32)

    def remote(src, dst, send, recv, axis, step):
        return pltpu.make_async_remote_copy(
            src_ref=src, dst_ref=dst, send_sem=send, recv_sem=recv,
            device_id=to(axis, step), device_id_type=MESH,
        )

    def start(copies):
        for sends, _, copy in copies:
            @pl.when(sends)
            def _(copy=copy):
                copy.start()

    def arrive(copies):
        for _, receives, copy in copies:
            @pl.when(receives)
            def _(copy=copy):
                copy.wait_recv()

    def faces(axis, src, dst, send, recv):
        return [
            (has[axis][side], has[axis][1 - side], remote(
                src[side], dst.at[1 - side], send.at[side], recv.at[1 - side], axis, step))
            for side, step in enumerate((-1, 1))
        ]

    edges = (pl.ds(Y, Y), pl.ds(Y * X, Y))
    u_x = faces(0, [u_hbm.at[:, pl.ds(at, Y), :] for at in (0, N - Y)], xur, x_send, x_recv)
    u_y = faces(1, [u_rows.at[:, :, y, :] for y in (0, Y - 1)], yur, y_send, y_recv)
    u_z = faces(2, [zus, zus], zur, z_send, z_recv)
    totals_down = [
        (me[2] + d < layers, me[2] >= d, remote(
            zts, ztr.at[d - 1], t_send.at[d - 1], t_recv.at[d - 1], 2, d))
        for d in range(1, layers)
    ]

    pl.semaphore_wait(barrier, expected)
    start(u_x + u_y)
    loads[0].wait()
    message = plane
    for x in range(X):
        for c in range(3):
            q = c * X + x
            tile = pltpu.roll(uv[c, pl.ds(Y + x * Y, Y), :], (2 * q + 1) % Z, 1)
            message = jnp.where(pair == q, tile, message)
    zus[...] = message
    start(u_z)

    loads[1].wait()
    total_depth = Z * layers
    depth = (me[2] * Z + lax.broadcasted_iota(jnp.int32, (N, Z), 1)).astype(jnp.float32)
    weight = rv[...] * (1.0 + 2.0 * depth / total_depth) / total_depth
    above_row = lax.broadcasted_iota(jnp.int32, (Z, 2 * Z), 0)
    column = lax.broadcasted_iota(jnp.int32, (Z, 2 * Z), 1)
    triangle = jnp.where(
        (above_row < column) | (column >= Z),
        1.0,
        jnp.where(above_row == column, 0.5, 0.0),
    ).astype(jnp.float32)
    sums = jnp.dot(
        weight, triangle, precision=lax.Precision.HIGHEST, preferred_element_type=jnp.float32
    )
    pv[...] = sums[:, :Z] + 1.0
    totals = sums[:, Z:]
    message = plane
    for x in range(X):
        message = jnp.where(lane == x, totals[x * Y:(x + 1) * Y], message)
    zts[...] = message
    start(totals_down)

    for copy in loads[2:]:
        copy.wait()
    for x in range(X):
        base = Y + x * Y
        own = pl.ds(x * Y, Y)
        grad = []
        for c in range(3):
            here = uv[c, pl.ds(base, Y), :]
            grad.append((
                (uv[c, pl.ds(base + Y, Y), :] - uv[c, pl.ds(base - Y, Y), :]) * 0.5,
                uv[c, pl.ds(base + 1, Y), :] * not_last - uv[c, pl.ds(base - 1, Y), :] * not_first,
                pltpu.roll(here, Z - 1, 1) * z_last - pltpu.roll(here, 1, 1) * z_first,
            ))
        el[0, own, :] = grad[0][0] - ev[0, own, :]
        el[1, own, :] = grad[1][1] - ev[1, own, :]
        el[2, own, :] = grad[2][2] - ev[2, own, :]
        el[3, own, :] = 0.5 * (grad[0][1] + grad[1][0]) - ev[3, own, :]
        el[4, own, :] = 0.5 * (grad[0][2] + grad[2][0]) - ev[4, own, :]
        el[5, own, :] = 0.5 * (grad[1][2] + grad[2][1]) - ev[5, own, :]
        nt[own, :] = -2.0 / tv[own, :]

    arrive(u_y)
    for side, line in enumerate((0, Y - 1)):
        sign = 2.0 * side - 1.0

        @pl.when(has[1][side])
        def _(side=side, sign=sign, line=line):
            own = pl.ds(line, X, stride=Y)
            for c, (part, factor) in enumerate(((3, 0.25), (1, 0.5), (5, 0.25))):
                el[part, own, :] = el[part, own, :] + (sign * factor) * yur[side, c]

    arrive(u_z + totals_down)
    carried = plane
    for d in range(1, layers):
        carried = carried + ztr[d - 1]
    merged = merge(zur, Z)

    s_x = faces(0, [sp.at[pl.ds(0, 3), edge, :] for edge in edges], xsr, x2_send, x2_recv)
    s_y = faces(1, [yss.at[0], yss.at[1]], ysr, y2_send, y2_recv)
    s_z = faces(2, [zss, zss], zsr, z2_send, z2_recv)

    def evolve(e, load, own):
        trace = e[0] + e[1] + e[2]
        third = trace * (1.0 / 3.0)
        half = [e[0] - third, e[1] - third, e[2] - third, e[3], e[4], e[5]]
        second = half[0] * half[0] + half[1] * half[1] + half[2] * half[2]
        second = second + 2.0 * (half[3] * half[3] + half[4] * half[4] + half[5] * half[5])
        weak = 2.0 + 14.0 * bv[own, :].astype(jnp.float32)
        rate = weak * jnp.exp(load * nt[own, :]) * second
        e = list(e)
        for c in range(6):
            change = rate * half[c]
            fv[c, own, :] = ev[c, own, :] + change
            e[c] = e[c] - change
        trace = e[0] + e[1] + e[2]
        return [
            2.0 * e[0] + trace, 2.0 * e[4], 2.0 * e[3],
            2.0 * e[1] + trace, 2.0 * e[5], 2.0 * e[2] + trace,
        ]

    def advance(x, message):
        own = pl.ds(x * Y, Y)
        e = [el[c, own, :] for c in range(6)]
        e[4] = e[4] + 0.5 * edge_term(merged, x, z_edge)
        e[5] = e[5] + 0.5 * edge_term(merged, X + x, z_edge)
        e[2] = e[2] + edge_term(merged, 2 * X + x, z_edge)
        load = pv[own, :] + jnp.broadcast_to(carried[:, x:x + 1], (Y, Z))
        stress = evolve(e, load, own)
        for c in range(6):
            sp[c, pl.ds(Y + x * Y, Y), :] = stress[c]
        for c in range(3):
            q = c * X + x
            tile = pltpu.roll(stress[Z_SET[c]], (2 * q + 1) % Z, 1)
            message = jnp.where(pair == q, tile, message)
        return message

    message = plane
    for x in range(1, X - 1):
        message = advance(x, message)
    arrive(u_x)
    for side, at in enumerate((0, X - 1)):
        sign = 2.0 * side - 1.0

        @pl.when(has[0][side])
        def _(side=side, sign=sign, at=at):
            own = pl.ds(at * Y, Y)
            for c, (part, factor) in enumerate(((0, 0.5), (3, 0.25), (4, 0.25))):
                el[part, own, :] = el[part, own, :] + (sign * factor) * xur[side, c]

    for x in sorted({0, X - 1}):
        message = advance(x, message)
    start(s_x)
    zss[...] = message
    start(s_z)
    for side, line in enumerate((0, Y - 1)):
        for c in range(3):
            yss[side, c] = sp[Y_SET[c], pl.ds(Y + line, X, stride=Y), :]
    start(s_y)

    for x in range(X):
        base = Y + x * Y
        own = pl.ds(x * Y, Y)
        for c in range(3):
            cx, cy, cz = X_SET[c], Y_SET[c], Z_SET[c]
            here = sp[cz, pl.ds(base, Y), :]
            total = (sp[cx, pl.ds(base + Y, Y), :] - sp[cx, pl.ds(base - Y, Y), :]) * 0.5
            total = total + (
                sp[cy, pl.ds(base + 1, Y), :] * not_last - sp[cy, pl.ds(base - 1, Y), :] * not_first
            )
            total = total + (pltpu.roll(here, Z - 1, 1) * z_last - pltpu.roll(here, 1, 1) * z_first)
            if c == 2:
                total = total - 0.5 * rv[own, :]
            mv[c, own, :] = total

    arrive(s_y)
    for side, line in enumerate((0, Y - 1)):
        @pl.when(has[1][side])
        def _(side=side, line=line):
            own = pl.ds(line, X, stride=Y)
            for c in range(3):
                mv[c, own, :] = mv[c, own, :] + (side - 0.5) * ysr[side, c]

    arrive(s_z)
    merged = merge(zsr, Z)
    for c in range(3):
        for x in range(X):
            own = pl.ds(x * Y, Y)
            mv[c, own, :] = mv[c, own, :] + edge_term(merged, c * X + x, z_edge)

    for sends, _, copy in u_x + u_y + u_z + totals_down + s_y + s_z:
        @pl.when(sends)
        def _(copy=copy):
            copy.wait_send()

    arrive(s_x)
    for side, at in enumerate((0, X - 1)):
        @pl.when(has[0][side])
        def _(side=side, at=at):
            own = pl.ds(at * Y, Y)
            for c in range(3):
                mv[c, own, :] = mv[c, own, :] + (side - 0.5) * xsr[side, X_SET[c]]

    for sends, _, copy in s_x:
        @pl.when(sends)
        def _(copy=copy):
            copy.wait_send()


def finish(fv, mv, f_hbm, m_hbm, sem):
    copies = [
        pltpu.make_async_copy(mv, m_hbm, sem.at[0]),
        pltpu.make_async_copy(fv, f_hbm, sem.at[1]),
    ]
    for copy in copies:
        copy.start()
    for copy in copies:
        copy.wait()


def shards(sizes, u, e, t, r, b):
    X, Y, Z = t.shape
    N = X * Y
    layers = sizes[2]
    assert 8 * X <= Z and Z % 128 == 0 and Y % 8 == 0
    f32 = jnp.float32
    vmem = pltpu.VMEM
    dma = pltpu.SemaphoreType.DMA
    any_space = pl.BlockSpec(memory_space=pl.ANY)
    in_vmem = pl.BlockSpec(memory_space=vmem)
    pair_sem = dma((2,))
    per_layer = dma((max(layers - 1, 1),))
    kept = pl.pallas_call(
        functools.partial(kernel, (X, Y, Z), sizes),
        out_shape=(vmem((6, N, Z), f32), vmem((3, N, Z), f32)),
        in_specs=[any_space] * 6,
        out_specs=(in_vmem, in_vmem),
        scratch_shapes=[
            vmem((3, N + 2 * Y, Z), f32),
            vmem((6, N, Z), f32),
            vmem((N, Z), f32),
            vmem((N, Z), f32),
            vmem((N, Z), jnp.int32),
            vmem((N, Z), f32),
            vmem((6, N, Z), f32),
            vmem((N, Z), f32),
            vmem((6, N + 2 * Y, Z), f32),
            vmem((2, 3, X, Z), f32),
            vmem((Y, Z), f32),
            vmem((2, Y, Z), f32),
            vmem((Y, Z), f32),
            vmem((max(layers - 1, 1), Y, Z), f32),
            vmem((2, 3, Y, Z), f32),
            vmem((2, 3, X, Z), f32),
            vmem((2, 3, X, Z), f32),
            vmem((Y, Z), f32),
            vmem((2, Y, Z), f32),
            vmem((2, 3, Y, Z), f32),
            dma((5,)),
        ] + [pair_sem] * 6 + [per_layer] * 2 + [pair_sem] * 6,
        compiler_params=pltpu.CompilerParams(collective_id=0, has_side_effects=True),
        name="strain_step",
    )(
        u.reshape(3, N, Z), u, e.reshape(6, N, Z), t.reshape(N, Z), r.reshape(N, Z), b.reshape(N, Z)
    )
    f, m = pl.pallas_call(
        finish,
        out_shape=(jax.ShapeDtypeStruct((6, N, Z), f32), jax.ShapeDtypeStruct((3, N, Z), f32)),
        in_specs=[in_vmem] * 2,
        out_specs=(any_space, any_space),
        scratch_shapes=[pair_sem],
        name="finish",
    )(*(pltpu.with_memory_space_constraint(k, vmem) for k in kept))
    return f.reshape(6, X, Y, Z), m.reshape(3, X, Y, Z)


def solution(mesh):
    sizes = tuple(mesh.shape[a] for a in AXES)
    field = P("gx", "gy", "gz")
    fields = P(None, "gx", "gy", "gz")
    return jax.shard_map(
        functools.partial(shards, sizes),
        mesh=mesh,
        in_specs=(fields, fields, field, field, field),
        out_specs=(fields, fields),
        check_vma=False,
    )
```
